128 devices in a mesh: row: 8 (over y_lo, z), col: 16 (over y_hi, x, core).
Axes of the slice: x: 4, y: 4 (y_hi: 2, y_lo: 2; y = y_hi * 2 + y_lo), z: 4, core: 2. Of those that a mesh axis runs over, the one named last changes fastest.
Arguments:
- amplitudes: bfloat16 [16384, 16384], P('row', 'col'), may hold values from -0.046875 to 0.046875
- accumulated: float32 [16384, 16384], P('row', 'col'), may hold values from -6 to 6
- cholesky: bfloat16 [16384, 1536], P(('row', 'col')), may hold values from -1.5 to 1.5
- occ_index: int32 [16384], replicated, may hold values from 0 to 63
- vir_index: int32 [16384], replicated, may hold values from 0 to 255
- occ_energy: float32 [64], replicated, may hold values from -3 to -0.5
- vir_energy: float32 [256], replicated, may hold values from 0.5 to 4
Outputs:
- updated: float32 [16384, 16384], P('row', 'col')
The draws below stay inside these ranges and needn't reach their ends.
All inputs are finite; a program needn't handle non-finite values.
Results may differ from the reference program's by a relative error of at most 0.0022.
Values may be sent and summed in bfloat16 or wider, within the bound.
No kernel may reach another device: no remote copies, remote signals or barrier semaphores. Data moves between devices by JAX's collectives and lax.ppermute only.
A program may use at most 128 MiB of HBM per device.

```python
import jax
import jax.numpy as jnp
from jax import lax

N = 16384
P_SIZE = 1536
NOCC = 64
NVIR = 256


def place_ends(values, key, smallest, largest):
    place = [jax.random.randint(jax.random.fold_in(key, axis), (), 0, length) for axis, length in enumerate(values.shape)]
    longest = values.shape.index(max(values.shape))
    beside = place[:longest] + [(place[longest] + 1) % values.shape[longest]] + place[longest + 1:]
    return values.at[tuple(place)].set(smallest).at[tuple(beside)].set(largest)


def levels(rng, shape, split, smallest, high):
    gain, own = 1.0, jax.random.fold_in(rng, 6)
    for axis_at, parts in split:
        steps = jnp.exp(jax.random.uniform(jax.random.fold_in(own, axis_at), (parts,), jnp.float32, smallest / len(split), high / len(split)))
        gain = gain * jnp.repeat(steps, shape[axis_at] // parts).reshape([-1 if axis == axis_at else 1 for axis in range(len(shape))])
    return gain


def noise(own_key, dims, width, most, shards=(), held_as=jnp.bfloat16):
    values = jax.random.normal(own_key, dims, jnp.float32) * width
    if len(shards) > 0:
        values = levels(own_key, dims, shards, -0.22, 0.18) * values
    return jnp.clip(values, min=-most, max=most).astype(held_as)


def setup_inputs(seed: int = 0) -> dict:
    splits = jax.random.split(jax.random.key(seed), 8)
    return {
        "amplitudes": noise(splits[0], (N, N), N ** -0.5, 0.046875, ((0, 8), (1, 16))),
        "accumulated": noise(splits[1], (N, N), 1.0, 6.0, ((0, 8), (1, 16)), jnp.float32),
        "cholesky": noise(splits[2], (N, P_SIZE), 0.25, 1.5, ((0, 128),)),
        "occ_index": place_ends(jax.random.randint(splits[3], (N,), 0, NOCC), jax.random.fold_in(splits[3], 1), 0, NOCC - 1).astype(jnp.int32),
        "vir_index": place_ends(jax.random.randint(splits[4], (N,), 0, NVIR), jax.random.fold_in(splits[4], 1), 0, NVIR - 1).astype(jnp.int32),
        "occ_energy": jnp.clip(jax.random.uniform(splits[5], (NOCC,), jnp.float32, -3.0, -0.5), -3.0, -0.5),
        "vir_energy": jnp.clip(jax.random.uniform(splits[6], (NVIR,), jnp.float32, 0.5, 4.0), 0.5, 4.0),
    }


def lookup(index, table):
    hits = index[:, None] == jnp.arange(table.shape[0], dtype=jnp.int32)[None, :]
    return jnp.sum(jnp.where(hits, table[None, :], jnp.zeros((), table.dtype)), axis=1)


def reference(amplitudes, accumulated, cholesky, occ_index, vir_index, occ_energy, vir_energy):
    tb = jnp.dot(amplitudes, cholesky, preferred_element_type=jnp.float32)
    dressed = (cholesky.astype(jnp.float32) + tb).astype(jnp.bfloat16)
    gap = lookup(occ_index, occ_energy) - lookup(vir_index, vir_energy)
    blocks = 16
    block_rows = N // blocks
    acc_blocks = accumulated.reshape(blocks, block_rows, N)
    x_blocks = dressed.reshape(blocks, block_rows, P_SIZE)
    gap_blocks = gap.reshape(blocks, block_rows)

    def one_block(items):
        acc_part, x_part, gap_part = items
        product = lax.dot_general(x_part, dressed, (((1,), (1,)), ((), ())), preferred_element_type=jnp.float32)
        return acc_part + product / (gap_part[:, None] + gap[None, :])

    result = lax.map(one_block, (acc_blocks, x_blocks, gap_blocks))
    return result.reshape(N, N)
```

```python
import functools

import jax
import jax.numpy as jnp
from jax import lax
from jax.experimental import pallas as pl
from jax.experimental.pallas import tpu as pltpu
from jax.sharding import PartitionSpec as P

CHUNKS = 3
SCALE = 64.0

PLACES = [(x, h, l, z, c) for x in range(4) for h in range(2) for l in range(2) for z in range(4) for c in range(2)]


def index_of(x, h, l, z, c):
    return (l * 4 + z % 4) * 16 + (h * 4 + x % 4) * 2 + c


def send(value, to):
    return lax.ppermute(value, ("row", "col"), [(index_of(*p), index_of(*to(*p))) for p in PLACES])


def other_core(x, h, l, z, c):
    return x, h, l, z, 1 - c


def other_h(x, h, l, z, c):
    return x, 1 - h, l, z, c


def other_l(x, h, l, z, c):
    return x, h, 1 - l, z, c


def along_x(step):
    return lambda x, h, l, z, c: (x + step, h, l, z, c)


def along_z(step):
    return lambda x, h, l, z, c: (x, h, l, z + step, c)


def skew(x, h, l, z, c):
    return x, h, l, z + x, c


def reflect(x, h, l, z, c):
    return z - x, l, h, z, c


STEPS = (0, 1, -1, 2)


def gather(piece, swap, along, forward):
    pieces = []
    for base in (piece, send(piece, swap)):
        ahead = send(base, along(-1))
        behind = send(base, along(1))
        if forward == 0:
            across = send(base, along(2))
        elif forward > 0:
            across = send(behind, along(1))
        else:
            across = send(ahead, along(-1))
        pieces += [base, ahead, behind, across]
    return pieces


def first_kernel(meta, own_ref, other_ref, *refs):
    pieces, outs, held = refs[:8], refs[8:12], refs[12]
    step = pl.program_id(0)
    rows, width = pieces[0].shape

    @pl.when(step == 0)
    def _():
        for i in range(8):
            held[pl.ds(pl.multiple_of(meta[8 + i] * rows, rows), rows), :] = pieces[i][...]

    half = 4 * rows
    value = jnp.dot(own_ref[...], held[:half, :], preferred_element_type=jnp.float32)
    value += jnp.dot(other_ref[...], held[half:, :], preferred_element_type=jnp.float32)
    for i in range(4):

        @pl.when(step // 2 == i)
        def _():
            outs[i][0] = value


def first_product(meta, own, other, pieces):
    rows, width = pieces[0].shape
    depth = own.shape[1]

    def out_spec(i):
        return pl.BlockSpec((1, rows, width), lambda j, m: (jnp.clip(j - 2 * i, 0, 1), 0, 0))

    t_spec = pl.BlockSpec((rows, depth), lambda j, m: (m[j], 0))
    return pl.pallas_call(
        first_kernel,
        out_shape=[jax.ShapeDtypeStruct((2, rows, width), jnp.float32)] * 4,
        grid_spec=pltpu.PrefetchScalarGridSpec(
            num_scalar_prefetch=1,
            grid=(8,),
            in_specs=[t_spec, t_spec] + [pl.BlockSpec((rows, width), lambda j, m: (0, 0))] * 8,
            out_specs=[out_spec(i) for i in range(4)],
            scratch_shapes=[pltpu.VMEM((8 * rows, width), jnp.bfloat16)],
        ),
        cost_estimate=pl.CostEstimate(
            flops=2 * 8 * rows * 2 * depth * width,
            bytes_accessed=8 * rows * (4 * depth + 6 * width),
            transcendentals=0,
        ),
        name="first",
    )(meta, own, other, *pieces)


def order_rows_kernel(meta, *refs):
    pieces, out = refs[:8], refs[8]
    rows = pieces[0].shape[0]
    for i in range(8):
        out[pl.ds(pl.multiple_of(meta[16 + i] * rows, rows), rows), :] = pieces[i][...]


def order_cols_kernel(meta, *refs):
    pieces, keep, give, held = refs[:8], refs[8], refs[9], refs[10]
    rows = pieces[0].shape[0]
    for i in range(8):
        held[pl.ds(pl.multiple_of(meta[8 + i] * rows, rows), rows), :] = pieces[i][...]
    keep[...] = held[: 4 * rows, :]
    give[...] = held[4 * rows :, :]


def order_rows(meta, pieces):
    rows, width = pieces[0].shape
    spec = pl.BlockSpec(memory_space=pltpu.VMEM)
    return pl.pallas_call(
        order_rows_kernel,
        out_shape=jax.ShapeDtypeStruct((8 * rows, width), jnp.bfloat16),
        grid_spec=pltpu.PrefetchScalarGridSpec(
            num_scalar_prefetch=1, grid=(), in_specs=[spec] * 8, out_specs=spec
        ),
        cost_estimate=pl.CostEstimate(flops=0, bytes_accessed=32 * rows * width, transcendentals=0),
        name="order_rows",
    )(meta, *pieces)


def order_cols(meta, pieces):
    rows, width = pieces[0].shape
    spec = pl.BlockSpec(memory_space=pltpu.VMEM)
    return pl.pallas_call(
        order_cols_kernel,
        out_shape=[jax.ShapeDtypeStruct((4 * rows, width), jnp.bfloat16)] * 2,
        grid_spec=pltpu.PrefetchScalarGridSpec(
            num_scalar_prefetch=1,
            grid=(),
            in_specs=[spec] * 8,
            out_specs=[spec, spec],
            scratch_shapes=[pltpu.VMEM((8 * rows, width), jnp.bfloat16)],
        ),
        cost_estimate=pl.CostEstimate(flops=0, bytes_accessed=32 * rows * width, transcendentals=0),
        name="order_cols",
    )(meta, *pieces)


def second_kernel(count, acc_ref, gap_rows_ref, gap_cols_ref, *refs):
    row_refs, col_refs, out_ref, held = refs[:count], refs[count : 2 * count], refs[2 * count], refs[2 * count + 1]
    width = col_refs[0].shape[1]

    @pl.when(pl.program_id(0) == 0)
    def _():
        for i in range(count):
            held[:, i * width : (i + 1) * width] = col_refs[i][...]

    left = jnp.concatenate([r[...] for r in row_refs], axis=1)
    product = lax.dot_general(left, held[...], (((1,), (1,)), ((), ())), preferred_element_type=jnp.float32)
    out_ref[...] = acc_ref[...] + product / (gap_rows_ref[...] + gap_cols_ref[...])


def second_product(accumulated, gap_rows, gap_cols, row_parts, col_parts):
    rows, cols = accumulated.shape
    width = row_parts[0].shape[1]
    count = len(row_parts)
    block = 256
    return pl.pallas_call(
        functools.partial(second_kernel, count),
        out_shape=jax.ShapeDtypeStruct((rows, cols), jnp.float32),
        grid=(rows // block,),
        in_specs=[
            pl.BlockSpec((block, cols), lambda i: (i, 0)),
            pl.BlockSpec((block, 1), lambda i: (i, 0)),
            pl.BlockSpec((1, cols), lambda i: (0, 0)),
        ]
        + [pl.BlockSpec((block, width), lambda i: (i, 0))] * count
        + [pl.BlockSpec((cols, width), lambda i: (0, 0))] * count,
        out_specs=pl.BlockSpec((block, cols), lambda i: (i, 0)),
        scratch_shapes=[pltpu.VMEM((cols, count * width), jnp.bfloat16)],
        cost_estimate=pl.CostEstimate(
            flops=2 * rows * cols * count * width,
            bytes_accessed=rows * cols * 8 + 2 * (rows + cols) * count * width,
            transcendentals=0,
        ),
        name="second",
    )(accumulated, gap_rows[:, None], gap_cols[None, :], *row_parts, *col_parts)


def lookup(index, table):
    hits = index[:, None] == jnp.arange(table.shape[0], dtype=jnp.int32)[None, :]
    return jnp.sum(jnp.where(hits, table[None, :], jnp.zeros((), table.dtype)), axis=1)


def narrow(value):
    return (value * SCALE).astype(jnp.float16)


def widen(value):
    return value.astype(jnp.float32) * (1.0 / SCALE)


def on_device(amplitudes, accumulated, cholesky, occ_index, vir_index, occ_energy, vir_energy):
    row_rank = lax.axis_index("row").astype(jnp.int32)
    col_rank = lax.axis_index("col").astype(jnp.int32)
    row_block, col_block = amplitudes.shape
    l, z = row_rank >> 2, row_rank & 3
    h, x, c = col_rank >> 3, (col_rank >> 1) & 3, col_rank & 1

    swap = jnp.array([0, 0, 0, 0, 1, 1, 1, 1], jnp.int32)
    ring = jnp.array(STEPS + STEPS, jnp.int32)
    alternate = jnp.array([0, 1] * 4, jnp.int32)
    offset = jnp.array([0, 0, 1, 1, 2, 2, 3, 3], jnp.int32)
    destinations = (h ^ alternate) * 4 + ((x + offset) & 3)
    sources = ((l ^ swap) * 4 + ((z + ring - x) & 3) - 4 * c) & 7
    mine = (h ^ swap) * 4 + ((x + ring) & 3)
    meta = jnp.concatenate([destinations, sources, mine])

    half = cholesky.shape[1] // 2
    low, high = cholesky[:, :half], cholesky[:, half:]
    keep = jnp.where(c == 0, low, high)
    got = send(jnp.where(c == 0, high, low), other_core)
    first = jnp.where(c == 0, keep, got)
    second = jnp.where(c == 0, got, keep)
    amplitudes_other = send(amplitudes, other_core)

    width = half // CHUNKS
    row_parts, col_parts, row_others, col_others = [], [], [], []
    for j in range(CHUNKS):
        forward = (1, -1)[j % 2]
        columns = slice(j * width, (j + 1) * width)
        b_piece = jnp.concatenate([first[:, columns], second[:, columns]], axis=0)
        b_pieces = gather(send(send(b_piece, skew), reflect), other_l, along_z, forward)
        partials = first_product(meta, amplitudes, amplitudes_other, b_pieces)
        arrived = [send(narrow(partials[s]), along_x(s)) for s in (1, 2, 3)]
        total = partials[0] + sum(widen(a) for a in arrived)
        rest = send(narrow(total[1]), other_h)
        x_piece = (b_piece.astype(jnp.float32) + (total[0] + widen(rest))).astype(jnp.bfloat16)
        col_pieces = gather(send(send(x_piece, skew), reflect), other_l, along_z, forward)
        row_pieces = gather(x_piece, other_h, along_x, forward)
        x_rows = order_rows(meta, row_pieces)
        x_cols, x_cols_give = order_cols(meta, col_pieces)
        row_parts.append(x_rows)
        row_others.append(send(x_rows, other_core))
        col_parts.append(x_cols)
        col_others.append(send(x_cols_give, other_core))

    occ_rows = lax.dynamic_slice_in_dim(occ_index, row_rank * row_block, row_block, 0)
    vir_rows = lax.dynamic_slice_in_dim(vir_index, row_rank * row_block, row_block, 0)
    occ_cols = lax.dynamic_slice_in_dim(occ_index, col_rank * col_block, col_block, 0)
    vir_cols = lax.dynamic_slice_in_dim(vir_index, col_rank * col_block, col_block, 0)
    gap_rows = lookup(occ_rows, occ_energy) - lookup(vir_rows, vir_energy)
    gap_cols = lookup(occ_cols, occ_energy) - lookup(vir_cols, vir_energy)
    return second_product(accumulated, gap_rows, gap_cols, row_parts + row_others, col_parts + col_others)


def solution(mesh):
    in_specs = (P("row", "col"), P("row", "col"), P(("row", "col"), None), P(), P(), P(), P())
    out_specs = P("row", "col")
    return jax.shard_map(
        on_device, mesh=mesh, in_specs=in_specs, out_specs=out_specs, check_vma=False
    )
```

```python
import functools

import jax
import jax.numpy as jnp
from jax import lax
from jax.experimental import pallas as pl
from jax.experimental.pallas import tpu as pltpu
from jax.sharding import PartitionSpec as P


WIDTHS = (256, 512)
ORDER = "SsRrYyQq*FfPpXUxONuZWnowzGVvgEe"
SCALE = 64.0

PLACES = [(x, h, l, z, c) for x in range(4) for h in range(2) for l in range(2) for z in range(4) for c in range(2)]


def index_of(x, h, l, z, c):
    return (l * 4 + z % 4) * 16 + (h * 4 + x % 4) * 2 + c


def send(value, to):
    pairs = [(index_of(*p), index_of(*to(*p))) for p in PLACES if to(*p) is not None]
    return lax.ppermute(value, ("row", "col"), pairs)


def other_core(x, h, l, z, c):
    return x, h, l, z, 1 - c


def other_h(x, h, l, z, c):
    return x, 1 - h, l, z, c


def other_l(x, h, l, z, c):
    return x, h, 1 - l, z, c


def along_x(step):
    return lambda x, h, l, z, c: (x + step, h, l, z, c)


def along_z(step):
    return lambda x, h, l, z, c: (x, h, l, z + step, c)


def along_col(swap, step):
    return lambda x, h, l, z, c: (x + step, h ^ swap, l, z, c)


def skew(x, h, l, z, c):
    return x, h, l, z + x, c


def reflect(x, h, l, z, c):
    return z - x, l, h, z, c


def pass_core(x, h, l, z, c):
    return (x, h, l, z, 1 - c) if l != c else (x, h, 1 - l, z, c)


def cross_core(x, h, l, z, c):
    return (x, h, 1 - l, z, 1 - c) if l != c else None


RING = (0, 1, -1, 2)
SWAP_RING = [(s, r) for s in (0, 1) for r in RING]
TARGETS = [(1, 2), (1, 1), (1, -1), (1, 0), (0, 2), (0, 1), (0, -1), (0, 0)]


def near_sends(base, along):
    return [send(base, along(-1)), send(base, along(1))]


def first_kernel(meta, *refs):
    lefts, pieces, out, held = refs[:4], refs[4:12], refs[12], refs[13]
    rows = pieces[0].shape[0]

    @pl.when(pl.program_id(0) == 0)
    def _():
        for i in range(8):
            held[pl.ds(pl.multiple_of(meta[8 + i] * rows, rows), rows), :] = pieces[i][...]

    own = jnp.concatenate([lefts[0][...], lefts[1][...]], axis=0)
    other = jnp.concatenate([lefts[2][...], lefts[3][...]], axis=0)
    left = jnp.concatenate([own, other], axis=1)
    value = jnp.dot(left, held[...], preferred_element_type=jnp.float32)
    out[0] = value[:rows]
    out[1] = value[rows:]


def first_product(meta, own, other, pieces):
    rows, width = pieces[0].shape
    depth = own.shape[1]
    even = pl.BlockSpec((rows, depth), lambda j, m: (m[2 * j], 0))
    odd = pl.BlockSpec((rows, depth), lambda j, m: (m[2 * j + 1], 0))
    return pl.pallas_call(
        first_kernel,
        out_shape=jax.ShapeDtypeStruct((8, rows, width), jnp.float32),
        grid_spec=pltpu.PrefetchScalarGridSpec(
            num_scalar_prefetch=1,
            grid=(4,),
            in_specs=[even, odd, even, odd] + [pl.BlockSpec((rows, width), lambda j, m: (0, 0))] * 8,
            out_specs=pl.BlockSpec((2, rows, width), lambda j, m: (j, 0, 0)),
            scratch_shapes=[pltpu.VMEM((8 * rows, width), jnp.bfloat16)],
        ),
        cost_estimate=pl.CostEstimate(
            flops=2 * 8 * rows * 2 * depth * width,
            bytes_accessed=8 * rows * (4 * depth + 6 * width),
            transcendentals=0,
        ),
        name="first",
    )(meta, own, own, other, other, *pieces)


def order_rows_kernel(meta, *refs):
    pieces, out = refs[:8], refs[8]
    rows = pieces[0].shape[0]
    for i in range(8):
        out[pl.ds(pl.multiple_of(meta[16 + i] * rows, rows), rows), :] = pieces[i][...]


def order_rows(meta, pieces):
    rows, width = pieces[0].shape
    spec = pl.BlockSpec(memory_space=pltpu.VMEM)
    return pl.pallas_call(
        order_rows_kernel,
        out_shape=jax.ShapeDtypeStruct((8 * rows, width), jnp.bfloat16),
        grid_spec=pltpu.PrefetchScalarGridSpec(
            num_scalar_prefetch=1, grid=(), in_specs=[spec] * 8, out_specs=spec
        ),
        cost_estimate=pl.CostEstimate(flops=0, bytes_accessed=32 * rows * width, transcendentals=0),
        name="order_rows",
    )(meta, *pieces)


def second_kernel(widths, meta, acc_ref, gap_rows_ref, gap_cols_ref, *refs):
    count = len(widths)
    row_refs, col_refs, out_ref, held = refs[:count], refs[count : 5 * count], refs[5 * count], refs[5 * count + 1]
    rows = col_refs[0].shape[0]

    @pl.when(pl.program_id(0) == 0)
    def _():
        start = 0
        for i in range(count):
            for r in range(4):
                place = pl.ds(pl.multiple_of(meta[24 + r] * rows, rows), rows)
                held[place, start : start + widths[i]] = col_refs[4 * i + r][...]
            start += widths[i]

    left = jnp.concatenate([r[...] for r in row_refs], axis=1)
    product = lax.dot_general(left, held[...], (((1,), (1,)), ((), ())), preferred_element_type=jnp.float32)
    out_ref[...] = acc_ref[...] + product / (gap_rows_ref[:, :1] + gap_cols_ref[...])


def second_product(meta, accumulated, gap_rows, gap_cols, row_parts, col_parts):
    rows, cols = accumulated.shape
    widths = [part.shape[1] for part in row_parts]
    depth = sum(widths)
    block = 512
    return pl.pallas_call(
        functools.partial(second_kernel, widths),
        out_shape=jax.ShapeDtypeStruct((rows, cols), jnp.float32),
        grid_spec=pltpu.PrefetchScalarGridSpec(
            num_scalar_prefetch=1,
            grid=(rows // block,),
            in_specs=[
                pl.BlockSpec((block, cols), lambda i, m: (i, 0)),
                pl.BlockSpec((block, 128), lambda i, m: (i, 0)),
                pl.BlockSpec((1, cols), lambda i, m: (0, 0)),
            ]
            + [pl.BlockSpec((block, width), lambda i, m: (i, 0)) for width in widths]
            + [pl.BlockSpec((cols // 4, width), lambda i, m: (0, 0)) for width in widths for _ in range(4)],
            out_specs=pl.BlockSpec((block, cols), lambda i, m: (i, 0)),
            scratch_shapes=[pltpu.VMEM((cols, depth), jnp.bfloat16)],
        ),
        cost_estimate=pl.CostEstimate(
            flops=2 * rows * cols * depth,
            bytes_accessed=rows * cols * 8 + 2 * (rows + cols) * depth,
            transcendentals=0,
        ),
        name="second",
    )(meta, accumulated, gap_rows, gap_cols, *row_parts, *col_parts)


def lookup(index, table):
    hits = index[:, None] == jnp.arange(table.shape[0], dtype=jnp.int32)[None, :]
    return jnp.sum(jnp.where(hits, table[None, :], jnp.zeros((), table.dtype)), axis=1)


def narrow(value):
    return (value * SCALE).astype(jnp.float16)


def widen(value):
    return value.astype(jnp.float32) * (1.0 / SCALE)


class Shared:
    pass


class Chunk:
    def __init__(self, env, b_piece):
        self.env, self.b_piece = env, b_piece

    def S(self):
        self.skewed = send(self.b_piece, skew)

    def R(self):
        self.base = send(self.skewed, reflect)

    def Y(self):
        self.swapped = send(self.base, other_l)
        self.near = near_sends(self.base, along_z)

    def Q(self):
        self.near_swapped = near_sends(self.swapped, along_z)

    def F(self):
        across = send(self.near[1], along_z(1))
        across_swapped = send(self.near_swapped[0], along_z(-1))
        self.b_pieces = [self.base, *self.near, across, self.swapped, *self.near_swapped, across_swapped]

    def P(self):
        self.partials = first_product(self.env.meta, self.env.own, self.env.other, self.b_pieces)
        self.arrived = [send(narrow(self.partials[i]), along_col(*TARGETS[i])) for i in range(7)]

    def X(self):
        total = self.partials[7] + sum(widen(a) for a in self.arrived)
        self.x_piece = (self.b_piece.astype(jnp.float32) + total).astype(jnp.bfloat16)
        self.skewed = send(self.x_piece, skew)
        self.swapped = send(self.x_piece, other_h)

    def O(self):
        self.near = near_sends(self.x_piece, along_x)

    def U(self):
        self.base = send(self.skewed, reflect)

    def W(self):
        self.near_swapped = near_sends(self.swapped, along_x)

    def V(self):
        across = send(self.near[1], along_x(1))
        across_swapped = send(self.near_swapped[0], along_x(-1))
        self.row_pieces = [self.x_piece, *self.near, across, self.swapped, *self.near_swapped, across_swapped]

    def N(self):
        near = send(self.base, pass_core)
        far = send(self.base, cross_core)
        straight = self.env.l == self.env.c
        self.mine = jnp.where(straight, self.base, near)
        self.theirs = jnp.where(straight, near, far)

    def Z(self):
        self.mine_near = near_sends(self.mine, along_z)
        self.theirs_near = near_sends(self.theirs, along_z)

    def G(self):
        mine_across = send(self.mine_near[1], along_z(1))
        theirs_across = send(self.theirs_near[0], along_z(-1))
        self.env.col_mine += [self.mine, *self.mine_near, mine_across]
        self.env.col_theirs += [self.theirs, *self.theirs_near, theirs_across]

    def E(self):
        x_rows = order_rows(self.env.meta, self.row_pieces)
        self.env.row_mine.append(x_rows)
        self.env.row_theirs.append(send(x_rows, other_core))


def on_device(amplitudes, accumulated, cholesky, occ_index, vir_index, occ_energy, vir_energy):
    row_rank = lax.axis_index("row").astype(jnp.int32)
    col_rank = lax.axis_index("col").astype(jnp.int32)
    row_block, col_block = amplitudes.shape
    l, z = row_rank >> 2, row_rank & 3
    h, x, c = col_rank >> 3, (col_rank >> 1) & 3, col_rank & 1
    env = Shared()
    env.l, env.c = l, c

    swap, ring = jnp.array(SWAP_RING, jnp.int32).T
    to_h, to_x = jnp.array(TARGETS, jnp.int32).T
    destinations = (h ^ to_h) * 4 + ((x + to_x) & 3)
    sources = ((l ^ swap) * 4 + ((z + ring - x) & 3) - 4 * c) & 7
    mine = (h ^ swap) * 4 + ((x + ring) & 3)
    env.meta = jnp.concatenate([destinations, sources, mine, (z + ring - x) & 3])

    half = cholesky.shape[1] // 2
    low, high = cholesky[:, :half], cholesky[:, half:]
    keep = jnp.where(c == 0, low, high)
    got = send(jnp.where(c == 0, high, low), other_core)
    b_piece = jnp.concatenate([jnp.where(c == 0, keep, got), jnp.where(c == 0, got, keep)], axis=0)
    env.own = amplitudes

    occ_rows = lax.dynamic_slice_in_dim(occ_index, row_rank * row_block, row_block, 0)
    vir_rows = lax.dynamic_slice_in_dim(vir_index, row_rank * row_block, row_block, 0)
    occ_cols = lax.dynamic_slice_in_dim(occ_index, col_rank * col_block, col_block, 0)
    vir_cols = lax.dynamic_slice_in_dim(vir_index, col_rank * col_block, col_block, 0)
    gap_rows = lookup(occ_rows, occ_energy) - lookup(vir_rows, vir_energy)
    gap_cols = lookup(occ_cols, occ_energy) - lookup(vir_cols, vir_energy)
    env.meta, gap_rows, gap_cols = lax.optimization_barrier(
        (env.meta, jnp.broadcast_to(gap_rows[:, None], (row_block, 128)), gap_cols[None, :])
    )

    env.row_mine, env.row_theirs, env.col_mine, env.col_theirs = [], [], [], []
    starts = [sum(WIDTHS[:j]) for j in range(len(WIDTHS))]
    chunks = [Chunk(env, b_piece[:, start : start + width]) for start, width in zip(starts, WIDTHS)]
    for stage in ORDER:
        if stage == "*":
            env.other = send(amplitudes, other_core)
        else:
            getattr(chunks[int(stage.islower())], stage.upper())()
    return second_product(
        env.meta, accumulated, gap_rows, gap_cols, env.row_mine + env.row_theirs, env.col_mine + env.col_theirs
    )


def solution(mesh):
    in_specs = (P("row", "col"), P("row", "col"), P(("row", "col"), None), P(), P(), P(), P())
    out_specs = P("row", "col")
    return jax.shard_map(on_device, mesh=mesh, in_specs=in_specs, out_specs=out_specs, check_vma=False)
```

```python
import functools

import jax
import jax.numpy as jnp
from jax import lax
from jax.experimental import pallas as pl
from jax.experimental.pallas import tpu as pltpu
from jax.sharding import PartitionSpec as P


WIDTHS = (256, 512)
ORDER = "SsRrYQ*yFqP+fMpmXUxONuZWnowzGVvgEe"
SCALE = 64.0

PLACES = [(x, h, l, z, c) for x in range(4) for h in range(2) for l in range(2) for z in range(4) for c in range(2)]


def index_of(x, h, l, z, c):
    return (l * 4 + z % 4) * 16 + (h * 4 + x % 4) * 2 + c


def send(value, to):
    pairs = [(index_of(*p), index_of(*to(*p))) for p in PLACES if to(*p) is not None]
    return lax.ppermute(value, ("row", "col"), pairs)


def other_core(x, h, l, z, c):
    return x, h, l, z, 1 - c


def other_h(x, h, l, z, c):
    return x, 1 - h, l, z, c


def other_l(x, h, l, z, c):
    return x, h, 1 - l, z, c


def along_x(step):
    return lambda x, h, l, z, c: (x + step, h, l, z, c)


def along_z(step):
    return lambda x, h, l, z, c: (x, h, l, z + step, c)


def along_col(swap, step):
    return lambda x, h, l, z, c: (x + step, h ^ swap, l, z, c)


def skew(x, h, l, z, c):
    return x, h, l, z + x, c


def reflect(x, h, l, z, c):
    return z - x, l, h, z, c


def pass_core(x, h, l, z, c):
    return (x, h, l, z, 1 - c) if l != c else (x, h, 1 - l, z, c)


def cross_core(x, h, l, z, c):
    return (x, h, 1 - l, z, 1 - c) if l != c else None


RING = (0, 1, -1, 2)
SWAP_RING = [(s, r) for s in (0, 1) for r in RING]
TARGETS = [(1, 2), (1, 1), (1, -1), (1, 0), (0, 2), (0, 1), (0, -1), (0, 0)]


def near_sends(base, along):
    return [send(base, along(-1)), send(base, along(1))]


def first_kernel(meta, *refs):
    lefts, pieces, out, held = refs[:4], refs[4:12], refs[12], refs[13]
    rows = pieces[0].shape[0]

    @pl.when(pl.program_id(0) == 0)
    def _():
        for i in range(8):
            held[pl.ds(pl.multiple_of(meta[8 + i] * rows, rows), rows), :] = pieces[i][...]

    own = jnp.concatenate([lefts[0][...], lefts[1][...]], axis=0)
    other = jnp.concatenate([lefts[2][...], lefts[3][...]], axis=0)
    left = jnp.concatenate([own, other], axis=1)
    value = jnp.dot(left, held[...], preferred_element_type=jnp.float32)
    out[0] = value[:rows]
    out[1] = value[rows:]


def first_product(meta, own, other, pieces):
    rows, width = pieces[0].shape
    depth = own.shape[1]
    even = pl.BlockSpec((rows, depth), lambda j, m: (m[2 * j], 0))
    odd = pl.BlockSpec((rows, depth), lambda j, m: (m[2 * j + 1], 0))
    return pl.pallas_call(
        first_kernel,
        out_shape=jax.ShapeDtypeStruct((8, rows, width), jnp.float32),
        grid_spec=pltpu.PrefetchScalarGridSpec(
            num_scalar_prefetch=1,
            grid=(4,),
            in_specs=[even, odd, even, odd] + [pl.BlockSpec((rows, width), lambda j, m: (0, 0))] * 8,
            out_specs=pl.BlockSpec((2, rows, width), lambda j, m: (j, 0, 0)),
            scratch_shapes=[pltpu.VMEM((8 * rows, width), jnp.bfloat16)],
        ),
        cost_estimate=pl.CostEstimate(
            flops=2 * 8 * rows * 2 * depth * width,
            bytes_accessed=8 * rows * (4 * depth + 6 * width),
            transcendentals=0,
        ),
        compiler_params=pltpu.CompilerParams(vmem_limit_bytes=20 << 20),
        name="first",
    )(meta, own, own, other, other, *pieces)


def order_rows_kernel(meta, *refs):
    pieces, out = refs[:8], refs[8]
    rows = pieces[0].shape[0]
    for i in range(8):
        out[pl.ds(pl.multiple_of(meta[16 + i] * rows, rows), rows), :] = pieces[i][...]


def order_rows(meta, pieces):
    rows, width = pieces[0].shape
    spec = pl.BlockSpec(memory_space=pltpu.VMEM)
    return pl.pallas_call(
        order_rows_kernel,
        out_shape=jax.ShapeDtypeStruct((8 * rows, width), jnp.bfloat16),
        grid_spec=pltpu.PrefetchScalarGridSpec(
            num_scalar_prefetch=1, grid=(), in_specs=[spec] * 8, out_specs=spec
        ),
        cost_estimate=pl.CostEstimate(flops=0, bytes_accessed=32 * rows * width, transcendentals=0),
        compiler_params=pltpu.CompilerParams(vmem_limit_bytes=12 << 20),
        name="order_rows",
    )(meta, *pieces)


def second_kernel(widths, meta, acc_ref, gap_rows_ref, gap_cols_ref, *refs):
    count = len(widths)
    row_refs, col_refs, out_ref, held = refs[:count], refs[count : 5 * count], refs[5 * count], refs[5 * count + 1]
    rows = col_refs[0].shape[0]

    @pl.when(pl.program_id(0) == 0)
    def _():
        start = 0
        for i in range(count):
            for r in range(4):
                place = pl.ds(pl.multiple_of(meta[24 + r] * rows, rows), rows)
                held[place, start : start + widths[i]] = col_refs[4 * i + r][...]
            start += widths[i]

    left = jnp.concatenate([r[...] for r in row_refs], axis=1)
    product = lax.dot_general(left, held[...], (((1,), (1,)), ((), ())), preferred_element_type=jnp.float32)
    out_ref[...] = acc_ref[...] + product / (gap_rows_ref[:, :1] + gap_cols_ref[...])


def second_product(meta, accumulated, gap_rows, gap_cols, row_parts, col_parts):
    rows, cols = accumulated.shape
    widths = [part.shape[1] for part in row_parts]
    depth = sum(widths)
    block = 512
    return pl.pallas_call(
        functools.partial(second_kernel, widths),
        out_shape=jax.ShapeDtypeStruct((rows, cols), jnp.float32),
        grid_spec=pltpu.PrefetchScalarGridSpec(
            num_scalar_prefetch=1,
            grid=(rows // block,),
            in_specs=[
                pl.BlockSpec((block, cols), lambda i, m: (i, 0)),
                pl.BlockSpec((block, 128), lambda i, m: (i, 0)),
                pl.BlockSpec((1, cols), lambda i, m: (0, 0)),
            ]
            + [pl.BlockSpec((block, width), lambda i, m: (i, 0)) for width in widths]
            + [pl.BlockSpec((cols // 4, width), lambda i, m: (0, 0)) for width in widths for _ in range(4)],
            out_specs=pl.BlockSpec((block, cols), lambda i, m: (i, 0)),
            scratch_shapes=[pltpu.VMEM((cols, depth), jnp.bfloat16)],
        ),
        cost_estimate=pl.CostEstimate(
            flops=2 * rows * cols * depth,
            bytes_accessed=rows * cols * 8 + 2 * (rows + cols) * depth,
            transcendentals=0,
        ),
        compiler_params=pltpu.CompilerParams(vmem_limit_bytes=32 << 20),
        name="second",
    )(meta, accumulated, gap_rows, gap_cols, *row_parts, *col_parts)


def lookup(index, table):
    hits = index[:, None] == jnp.arange(table.shape[0], dtype=jnp.int32)[None, :]
    return jnp.sum(jnp.where(hits, table[None, :], jnp.zeros((), table.dtype)), axis=1)


def narrow(value):
    return (value * SCALE).astype(jnp.float16)


def widen(value):
    return value.astype(jnp.float32) * (1.0 / SCALE)


class Shared:
    pass


class Chunk:
    def __init__(self, env, b_piece):
        self.env, self.b_piece = env, b_piece

    def S(self):
        self.skewed = send(self.b_piece, skew)

    def R(self):
        self.base = send(self.skewed, reflect)

    def Y(self):
        self.swapped = send(self.base, other_l)
        self.near = near_sends(self.base, along_z)

    def Q(self):
        self.near_swapped = near_sends(self.swapped, along_z)

    def F(self):
        across = send(self.near[1], along_z(1))
        across_swapped = send(self.near_swapped[0], along_z(-1))
        self.b_pieces = [self.base, *self.near, across, self.swapped, *self.near_swapped, across_swapped]

    def P(self):
        self.partials = first_product(self.env.meta, self.env.own, self.env.other, self.b_pieces)
        self.narrowed = [narrow(self.partials[i]) for i in range(7)]

    def M(self):
        self.arrived = [send(self.narrowed[i], along_col(*TARGETS[i])) for i in range(7)]

    def X(self):
        total = self.partials[7] + sum(widen(a) for a in self.arrived)
        self.x_piece = (self.b_piece.astype(jnp.float32) + total).astype(jnp.bfloat16)
        self.skewed = send(self.x_piece, skew)
        self.swapped = send(self.x_piece, other_h)

    def O(self):
        self.near = near_sends(self.x_piece, along_x)

    def U(self):
        self.base = send(self.skewed, reflect)

    def W(self):
        self.near_swapped = near_sends(self.swapped, along_x)

    def V(self):
        across = send(self.near[1], along_x(1))
        across_swapped = send(self.near_swapped[0], along_x(-1))
        self.row_pieces = [self.x_piece, *self.near, across, self.swapped, *self.near_swapped, across_swapped]

    def N(self):
        near = send(self.base, pass_core)
        far = send(self.base, cross_core)
        straight = self.env.l == self.env.c
        self.mine = jnp.where(straight, self.base, near)
        self.theirs = jnp.where(straight, near, far)

    def Z(self):
        self.mine_near = near_sends(self.mine, along_z)
        self.theirs_near = near_sends(self.theirs, along_z)

    def G(self):
        mine_across = send(self.mine_near[1], along_z(1))
        theirs_across = send(self.theirs_near[0], along_z(-1))
        self.env.col_mine += [self.mine, *self.mine_near, mine_across]
        self.env.col_theirs += [self.theirs, *self.theirs_near, theirs_across]

    def E(self):
        x_rows = order_rows(self.env.meta, self.row_pieces)
        self.env.row_mine.append(x_rows)
        self.env.row_theirs.append(send(x_rows, other_core))


def on_device(amplitudes, accumulated, cholesky, occ_index, vir_index, occ_energy, vir_energy):
    row_rank = lax.axis_index("row").astype(jnp.int32)
    col_rank = lax.axis_index("col").astype(jnp.int32)
    row_block, col_block = amplitudes.shape
    l, z = row_rank >> 2, row_rank & 3
    h, x, c = col_rank >> 3, (col_rank >> 1) & 3, col_rank & 1
    env = Shared()
    env.l, env.c = l, c

    swap, ring = jnp.array(SWAP_RING, jnp.int32).T
    to_h, to_x = jnp.array(TARGETS, jnp.int32).T
    destinations = (h ^ to_h) * 4 + ((x + to_x) & 3)
    sources = ((l ^ swap) * 4 + ((z + ring - x) & 3) - 4 * c) & 7
    mine = (h ^ swap) * 4 + ((x + ring) & 3)
    env.meta = jnp.concatenate([destinations, sources, mine, (z + ring - x) & 3])

    half = cholesky.shape[1] // 2
    low, high = cholesky[:, :half], cholesky[:, half:]
    keep = jnp.where(c == 0, low, high)
    got = send(jnp.where(c == 0, high, low), other_core)
    b_piece = jnp.concatenate([jnp.where(c == 0, keep, got), jnp.where(c == 0, got, keep)], axis=0)
    env.own = amplitudes

    occ_rows = lax.dynamic_slice_in_dim(occ_index, row_rank * row_block, row_block, 0)
    vir_rows = lax.dynamic_slice_in_dim(vir_index, row_rank * row_block, row_block, 0)
    occ_cols = lax.dynamic_slice_in_dim(occ_index, col_rank * col_block, col_block, 0)
    vir_cols = lax.dynamic_slice_in_dim(vir_index, col_rank * col_block, col_block, 0)
    gap_rows = lookup(occ_rows, occ_energy) - lookup(vir_rows, vir_energy)
    gap_cols = lookup(occ_cols, occ_energy) - lookup(vir_cols, vir_energy)
    env.meta, gap_rows, gap_cols = lax.optimization_barrier(
        (env.meta, jnp.broadcast_to(gap_rows[:, None], (row_block, 128)), gap_cols[None, :])
    )

    env.row_mine, env.row_theirs, env.col_mine, env.col_theirs = [], [], [], []
    starts = [sum(WIDTHS[:j]) for j in range(len(WIDTHS))]
    chunks = [Chunk(env, b_piece[:, start : start + width]) for start, width in zip(starts, WIDTHS)]
    for stage in ORDER:
        if stage == "*":
            env.other = send(amplitudes, other_core)
        elif stage == "+":
            tied = (chunks[0].narrowed, chunks[1].near, chunks[1].near_swapped)
            chunks[0].narrowed, chunks[1].near, chunks[1].near_swapped = lax.optimization_barrier(tied)
        else:
            getattr(chunks[int(stage.islower())], stage.upper())()
    return second_product(
        env.meta, accumulated, gap_rows, gap_cols, env.row_mine + env.row_theirs, env.col_mine + env.col_theirs
    )


def solution(mesh):
    in_specs = (P("row", "col"), P("row", "col"), P(("row", "col"), None), P(), P(), P(), P())
    out_specs = P("row", "col")
    return jax.shard_map(on_device, mesh=mesh, in_specs=in_specs, out_specs=out_specs, check_vma=False)
```

```python
import functools

import jax
import jax.numpy as jnp
from jax import lax
from jax.experimental import pallas as pl
from jax.experimental.pallas import tpu as pltpu
from jax.sharding import PartitionSpec as P


WIDTHS = (256, 512)
ORDER = "SsRrYQ*yFqP+fMpmXUxONuZWnowzVvGgEe"
SCALE = 64.0

PLACES = [(x, h, l, z, c) for x in range(4) for h in range(2) for l in range(2) for z in range(4) for c in range(2)]


def index_of(x, h, l, z, c):
    return (l * 4 + z % 4) * 16 + (h * 4 + x % 4) * 2 + c


def send(value, to):
    pairs = [(index_of(*p), index_of(*to(*p))) for p in PLACES if to(*p) is not None]
    return lax.ppermute(value, ("row", "col"), pairs)


def other_core(x, h, l, z, c):
    return x, h, l, z, 1 - c


def other_h(x, h, l, z, c):
    return x, 1 - h, l, z, c


def other_l(x, h, l, z, c):
    return x, h, 1 - l, z, c


def along_x(step):
    return lambda x, h, l, z, c: (x + step, h, l, z, c)


def along_z(step):
    return lambda x, h, l, z, c: (x, h, l, z + step, c)


def along_col(swap, step):
    return lambda x, h, l, z, c: (x + step, h ^ swap, l, z, c)


def skew(x, h, l, z, c):
    return x, h, l, z + x, c


def reflect(x, h, l, z, c):
    return z - x, l, h, z, c


def pass_core(x, h, l, z, c):
    return (x, h, l, z, 1 - c) if l != c else (x, h, 1 - l, z, c)


def cross_core(x, h, l, z, c):
    return (x, h, 1 - l, z, 1 - c) if l != c else None


RING = (0, 1, -1, 2)
SWAP_RING = [(s, r) for s in (0, 1) for r in RING]
TARGETS = [(1, 2), (1, 1), (1, -1), (1, 0), (0, 2), (0, 1), (0, -1), (0, 0)]


def near_sends(base, along):
    return [send(base, along(-1)), send(base, along(1))]


def first_kernel(meta, *refs):
    lefts, pieces, out, held = refs[:4], refs[4:12], refs[12], refs[13]
    rows = pieces[0].shape[0]

    @pl.when(pl.program_id(0) == 0)
    def _():
        for i in range(8):
            held[pl.ds(pl.multiple_of(meta[8 + i] * rows, rows), rows), :] = pieces[i][...]

    own = jnp.concatenate([lefts[0][...], lefts[1][...]], axis=0)
    other = jnp.concatenate([lefts[2][...], lefts[3][...]], axis=0)
    left = jnp.concatenate([own, other], axis=1)
    value = jnp.dot(left, held[...], preferred_element_type=jnp.float32)
    out[0] = value[:rows]
    out[1] = value[rows:]


def first_product(meta, own, other, pieces):
    rows, width = pieces[0].shape
    depth = own.shape[1]
    even = pl.BlockSpec((rows, depth), lambda j, m: (m[2 * j], 0))
    odd = pl.BlockSpec((rows, depth), lambda j, m: (m[2 * j + 1], 0))
    return pl.pallas_call(
        first_kernel,
        out_shape=jax.ShapeDtypeStruct((8, rows, width), jnp.float32),
        grid_spec=pltpu.PrefetchScalarGridSpec(
            num_scalar_prefetch=1,
            grid=(4,),
            in_specs=[even, odd, even, odd] + [pl.BlockSpec((rows, width), lambda j, m: (0, 0))] * 8,
            out_specs=pl.BlockSpec((2, rows, width), lambda j, m: (j, 0, 0)),
            scratch_shapes=[pltpu.VMEM((8 * rows, width), jnp.bfloat16)],
        ),
        cost_estimate=pl.CostEstimate(
            flops=2 * 8 * rows * 2 * depth * width,
            bytes_accessed=8 * rows * (4 * depth + 6 * width),
            transcendentals=0,
        ),
        compiler_params=pltpu.CompilerParams(vmem_limit_bytes=20 << 20),
        name="first",
    )(meta, *[pltpu.with_memory_space_constraint(own, pltpu.HBM)] * 2, other, other, *pieces)


def order_rows_kernel(meta, *refs):
    pieces, out = refs[:8], refs[8]
    rows = pieces[0].shape[0]
    for i in range(8):
        out[pl.ds(pl.multiple_of(meta[16 + i] * rows, rows), rows), :] = pieces[i][...]


def order_rows(meta, pieces):
    rows, width = pieces[0].shape
    spec = pl.BlockSpec(memory_space=pltpu.VMEM)
    return pl.pallas_call(
        order_rows_kernel,
        out_shape=jax.ShapeDtypeStruct((8 * rows, width), jnp.bfloat16),
        grid_spec=pltpu.PrefetchScalarGridSpec(
            num_scalar_prefetch=1, grid=(), in_specs=[spec] * 8, out_specs=spec
        ),
        cost_estimate=pl.CostEstimate(flops=0, bytes_accessed=32 * rows * width, transcendentals=0),
        compiler_params=pltpu.CompilerParams(vmem_limit_bytes=12 << 20),
        name="order_rows",
    )(meta, *pieces)


def second_kernel(widths, meta, acc_ref, gap_rows_ref, gap_cols_ref, *refs):
    count = len(widths)
    row_refs, col_refs, out_ref, held = refs[:count], refs[count : 5 * count], refs[5 * count], refs[5 * count + 1]
    rows = col_refs[0].shape[0]

    @pl.when(pl.program_id(0) == 0)
    def _():
        start = 0
        for i in range(count):
            for r in range(4):
                place = pl.ds(pl.multiple_of(meta[24 + r] * rows, rows), rows)
                held[place, start : start + widths[i]] = col_refs[4 * i + r][...]
            start += widths[i]

    left = jnp.concatenate([r[...] for r in row_refs], axis=1)
    product = lax.dot_general(left, held[...], (((1,), (1,)), ((), ())), preferred_element_type=jnp.float32)
    out_ref[...] = acc_ref[...] + product / (gap_rows_ref[:, :1] + gap_cols_ref[...])


def second_product(meta, accumulated, gap_rows, gap_cols, row_parts, col_parts):
    rows, cols = accumulated.shape
    widths = [part.shape[1] for part in row_parts]
    depth = sum(widths)
    block = 512
    return pl.pallas_call(
        functools.partial(second_kernel, widths),
        out_shape=jax.ShapeDtypeStruct((rows, cols), jnp.float32),
        grid_spec=pltpu.PrefetchScalarGridSpec(
            num_scalar_prefetch=1,
            grid=(rows // block,),
            in_specs=[
                pl.BlockSpec((block, cols), lambda i, m: (i, 0)),
                pl.BlockSpec((block, 128), lambda i, m: (i, 0)),
                pl.BlockSpec((1, cols), lambda i, m: (0, 0)),
            ]
            + [pl.BlockSpec((block, width), lambda i, m: (i, 0)) for width in widths]
            + [pl.BlockSpec((cols // 4, width), lambda i, m: (0, 0)) for width in widths for _ in range(4)],
            out_specs=pl.BlockSpec((block, cols), lambda i, m: (i, 0)),
            scratch_shapes=[pltpu.VMEM((cols, depth), jnp.bfloat16)],
        ),
        cost_estimate=pl.CostEstimate(
            flops=2 * rows * cols * depth,
            bytes_accessed=rows * cols * 8 + 2 * (rows + cols) * depth,
            transcendentals=0,
        ),
        compiler_params=pltpu.CompilerParams(vmem_limit_bytes=32 << 20),
        name="second",
    )(meta, pltpu.with_memory_space_constraint(accumulated, pltpu.HBM), gap_rows, gap_cols, *row_parts, *col_parts)


def lookup(index, table):
    hits = index[:, None] == jnp.arange(table.shape[0], dtype=jnp.int32)[None, :]
    return jnp.sum(jnp.where(hits, table[None, :], jnp.zeros((), table.dtype)), axis=1)


def narrow(value):
    return (value * SCALE).astype(jnp.float16)


def widen(value):
    return value.astype(jnp.float32) * (1.0 / SCALE)


class Shared:
    pass


class Chunk:
    def __init__(self, env, b_piece):
        self.env, self.b_piece = env, b_piece

    def S(self):
        self.skewed = send(self.b_piece, skew)

    def R(self):
        self.base = send(self.skewed, reflect)

    def Y(self):
        self.swapped = send(self.base, other_l)
        self.near = near_sends(self.base, along_z)

    def Q(self):
        self.near_swapped = near_sends(self.swapped, along_z)

    def F(self):
        across = send(self.near[1], along_z(1))
        across_swapped = send(self.near_swapped[0], along_z(-1))
        self.b_pieces = [self.base, *self.near, across, self.swapped, *self.near_swapped, across_swapped]

    def P(self):
        self.partials = first_product(self.env.meta, self.env.own, self.env.other, self.b_pieces)
        self.narrowed = [narrow(self.partials[i]) for i in range(7)]

    def M(self):
        self.arrived = [send(self.narrowed[i], along_col(*TARGETS[i])) for i in range(7)]

    def X(self):
        total = self.partials[7] + sum(widen(a) for a in self.arrived)
        self.x_piece = (self.b_piece.astype(jnp.float32) + total).astype(jnp.bfloat16)
        self.skewed = send(self.x_piece, skew)
        self.swapped = send(self.x_piece, other_h)

    def O(self):
        self.near = near_sends(self.x_piece, along_x)

    def U(self):
        self.base = send(self.skewed, reflect)

    def W(self):
        self.near_swapped = near_sends(self.swapped, along_x)

    def V(self):
        across = send(self.near[1], along_x(1))
        across_swapped = send(self.near_swapped[0], along_x(-1))
        self.row_pieces = [self.x_piece, *self.near, across, self.swapped, *self.near_swapped, across_swapped]

    def N(self):
        near = send(self.base, pass_core)
        far = send(self.base, cross_core)
        straight = self.env.l == self.env.c
        self.mine = jnp.where(straight, self.base, near)
        self.theirs = jnp.where(straight, near, far)

    def Z(self):
        self.mine_near = near_sends(self.mine, along_z)
        self.theirs_near = near_sends(self.theirs, along_z)

    def G(self):
        mine_across = send(self.mine_near[1], along_z(1))
        theirs_across = send(self.theirs_near[0], along_z(-1))
        self.env.col_mine += [self.mine, *self.mine_near, mine_across]
        self.env.col_theirs += [self.theirs, *self.theirs_near, theirs_across]

    def E(self):
        x_rows = order_rows(self.env.meta, self.row_pieces)
        self.env.row_mine.append(x_rows)
        self.env.row_theirs.append(send(x_rows, other_core))


def on_device(amplitudes, accumulated, cholesky, occ_index, vir_index, occ_energy, vir_energy):
    row_rank = lax.axis_index("row").astype(jnp.int32)
    col_rank = lax.axis_index("col").astype(jnp.int32)
    row_block, col_block = amplitudes.shape
    l, z = row_rank >> 2, row_rank & 3
    h, x, c = col_rank >> 3, (col_rank >> 1) & 3, col_rank & 1
    env = Shared()
    env.l, env.c = l, c

    swap, ring = jnp.array(SWAP_RING, jnp.int32).T
    to_h, to_x = jnp.array(TARGETS, jnp.int32).T
    destinations = (h ^ to_h) * 4 + ((x + to_x) & 3)
    sources = ((l ^ swap) * 4 + ((z + ring - x) & 3) - 4 * c) & 7
    mine = (h ^ swap) * 4 + ((x + ring) & 3)
    env.meta = jnp.concatenate([destinations, sources, mine, (z + ring - x) & 3])

    half = cholesky.shape[1] // 2
    low, high = cholesky[:, :half], cholesky[:, half:]
    keep = jnp.where(c == 0, low, high)
    got = send(jnp.where(c == 0, high, low), other_core)
    b_piece = jnp.concatenate([jnp.where(c == 0, keep, got), jnp.where(c == 0, got, keep)], axis=0)
    env.own = amplitudes

    occ_rows = lax.dynamic_slice_in_dim(occ_index, row_rank * row_block, row_block, 0)
    vir_rows = lax.dynamic_slice_in_dim(vir_index, row_rank * row_block, row_block, 0)
    occ_cols = lax.dynamic_slice_in_dim(occ_index, col_rank * col_block, col_block, 0)
    vir_cols = lax.dynamic_slice_in_dim(vir_index, col_rank * col_block, col_block, 0)
    gap_rows = lookup(occ_rows, occ_energy) - lookup(vir_rows, vir_energy)
    gap_cols = lookup(occ_cols, occ_energy) - lookup(vir_cols, vir_energy)
    env.meta, gap_rows, gap_cols = lax.optimization_barrier(
        (env.meta, jnp.broadcast_to(gap_rows[:, None], (row_block, 128)), gap_cols[None, :])
    )

    env.row_mine, env.row_theirs, env.col_mine, env.col_theirs = [], [], [], []
    starts = [sum(WIDTHS[:j]) for j in range(len(WIDTHS))]
    chunks = [Chunk(env, b_piece[:, start : start + width]) for start, width in zip(starts, WIDTHS)]
    for stage in ORDER:
        if stage == "*":
            env.other = send(amplitudes, other_core)
        elif stage == "+":
            tied = (chunks[0].narrowed, chunks[1].near, chunks[1].near_swapped)
            chunks[0].narrowed, chunks[1].near, chunks[1].near_swapped = lax.optimization_barrier(tied)
        else:
            getattr(chunks[int(stage.islower())], stage.upper())()
    return second_product(
        env.meta, accumulated, gap_rows, gap_cols, env.row_mine + env.row_theirs, env.col_mine + env.col_theirs
    )


def solution(mesh):
    in_specs = (P("row", "col"), P("row", "col"), P(("row", "col"), None), P(), P(), P(), P())
    out_specs = P("row", "col")
    return jax.shard_map(on_device, mesh=mesh, in_specs=in_specs, out_specs=out_specs, check_vma=False)
```

```python
import functools

import jax
import jax.numpy as jnp
from jax import lax
from jax.experimental import pallas as pl
from jax.experimental.pallas import tpu as pltpu
from jax.sharding import PartitionSpec as P


WIDTHS = (256, 512)
ORDER = "SsRrYQ*yFqP+fMpmXUxONuZWnowzVvGgEe"
SCALE = 64.0

PLACES = [(x, h, l, z, c) for x in range(4) for h in range(2) for l in range(2) for z in range(4) for c in range(2)]


def index_of(x, h, l, z, c):
    return (l * 4 + z % 4) * 16 + (h * 4 + x % 4) * 2 + c


def send(value, to):
    pairs = [(index_of(*p), index_of(*to(*p))) for p in PLACES if to(*p) is not None]
    return lax.ppermute(value, ("row", "col"), pairs)


def other_core(x, h, l, z, c):
    return x, h, l, z, 1 - c


def other_h(x, h, l, z, c):
    return x, 1 - h, l, z, c


def other_l(x, h, l, z, c):
    return x, h, 1 - l, z, c


def along_x(step):
    return lambda x, h, l, z, c: (x + step, h, l, z, c)


def along_z(step):
    return lambda x, h, l, z, c: (x, h, l, z + step, c)


def along_col(swap, step):
    return lambda x, h, l, z, c: (x + step, h ^ swap, l, z, c)


def skew(x, h, l, z, c):
    return x, h, l, z + x, c


def reflect(x, h, l, z, c):
    return z - x, l, h, z, c


def pass_core(x, h, l, z, c):
    return (x, h, l, z, 1 - c) if l != c else (x, h, 1 - l, z, c)


def cross_core(x, h, l, z, c):
    return (x, h, 1 - l, z, 1 - c) if l != c else None


RING = (0, 1, -1, 2)
SWAP_RING = [(s, r) for s in (0, 1) for r in RING]
TARGETS = [(1, 2), (1, 1), (1, -1), (1, 0), (0, 2), (0, 1), (0, -1), (0, 0)]


def near_sends(base, along):
    return [send(base, along(-1)), send(base, along(1))]


def first_kernel(meta, *refs):
    lefts, pieces, out, held = refs[:4], refs[4:12], refs[12], refs[13]
    rows = pieces[0].shape[0]

    @pl.when(pl.program_id(0) == 0)
    def _():
        for i in range(8):
            held[pl.ds(pl.multiple_of(meta[8 + i] * rows, rows), rows), :] = pieces[i][...]

    own = jnp.concatenate([lefts[0][...], lefts[1][...]], axis=0)
    other = jnp.concatenate([lefts[2][...], lefts[3][...]], axis=0)
    left = jnp.concatenate([own, other], axis=1)
    value = jnp.dot(left, held[...], preferred_element_type=jnp.float32)
    out[0] = value[:rows]
    out[1] = value[rows:]


def first_product(meta, own, other, pieces):
    rows, width = pieces[0].shape
    depth = own.shape[1]
    even = pl.BlockSpec((rows, depth), lambda j, m: (m[2 * j], 0))
    odd = pl.BlockSpec((rows, depth), lambda j, m: (m[2 * j + 1], 0))
    return pl.pallas_call(
        first_kernel,
        out_shape=jax.ShapeDtypeStruct((8, rows, width), jnp.float32),
        grid_spec=pltpu.PrefetchScalarGridSpec(
            num_scalar_prefetch=1,
            grid=(4,),
            in_specs=[even, odd, even, odd] + [pl.BlockSpec((rows, width), lambda j, m: (0, 0))] * 8,
            out_specs=pl.BlockSpec((2, rows, width), lambda j, m: (j, 0, 0)),
            scratch_shapes=[pltpu.VMEM((8 * rows, width), jnp.bfloat16)],
        ),
        cost_estimate=pl.CostEstimate(
            flops=2 * 8 * rows * 2 * depth * width,
            bytes_accessed=8 * rows * (4 * depth + 6 * width),
            transcendentals=0,
        ),
        compiler_params=pltpu.CompilerParams(vmem_limit_bytes=20 << 20),
        name="first",
    )(meta, *[pltpu.with_memory_space_constraint(own, pltpu.HBM)] * 2, other, other, *pieces)


def order_rows_kernel(meta, *refs):
    pieces, out = refs[:8], refs[8]
    rows = pieces[0].shape[0]
    for i in range(8):
        out[pl.ds(pl.multiple_of(meta[16 + i] * rows, rows), rows), :] = pieces[i][...]


def order_rows(meta, pieces):
    rows, width = pieces[0].shape
    spec = pl.BlockSpec(memory_space=pltpu.VMEM)
    return pl.pallas_call(
        order_rows_kernel,
        out_shape=jax.ShapeDtypeStruct((8 * rows, width), jnp.bfloat16),
        grid_spec=pltpu.PrefetchScalarGridSpec(
            num_scalar_prefetch=1, grid=(), in_specs=[spec] * 8, out_specs=spec
        ),
        cost_estimate=pl.CostEstimate(flops=0, bytes_accessed=32 * rows * width, transcendentals=0),
        compiler_params=pltpu.CompilerParams(vmem_limit_bytes=12 << 20),
        name="order_rows",
    )(meta, *pieces)


def second_kernel(widths, meta, acc_ref, gap_rows_ref, gap_cols_ref, *refs):
    count = len(widths)
    row_refs, col_refs, out_ref, held = refs[:count], refs[count : 5 * count], refs[5 * count], refs[5 * count + 1]
    rows = col_refs[0].shape[0]

    @pl.when(pl.program_id(0) == 0)
    def _():
        start = 0
        for i in range(count):
            for r in range(4):
                place = pl.ds(pl.multiple_of(meta[24 + r] * rows, rows), rows)
                held[place, start : start + widths[i]] = col_refs[4 * i + r][...]
            start += widths[i]

    left = jnp.concatenate([r[...] for r in row_refs], axis=1)
    product = lax.dot_general(left, held[...], (((1,), (1,)), ((), ())), preferred_element_type=jnp.float32)
    out_ref[...] = acc_ref[...] + product / (gap_rows_ref[:, :1] + gap_cols_ref[...])


def second_product(meta, accumulated, gap_rows, gap_cols, row_parts, col_parts):
    rows, cols = accumulated.shape
    widths = [part.shape[1] for part in row_parts]
    depth = sum(widths)
    block = 512
    return pl.pallas_call(
        functools.partial(second_kernel, widths),
        out_shape=jax.ShapeDtypeStruct((rows, cols), jnp.float32),
        grid_spec=pltpu.PrefetchScalarGridSpec(
            num_scalar_prefetch=1,
            grid=(rows // block,),
            in_specs=[
                pl.BlockSpec((block, cols), lambda i, m: (i, 0)),
                pl.BlockSpec((block, 128), lambda i, m: (i, 0)),
                pl.BlockSpec((1, cols), lambda i, m: (0, 0)),
            ]
            + [pl.BlockSpec((block, width), lambda i, m: (i, 0)) for width in widths]
            + [pl.BlockSpec((cols // 4, width), lambda i, m: (0, 0)) for width in widths for _ in range(4)],
            out_specs=pl.BlockSpec((block, cols), lambda i, m: (i, 0)),
            scratch_shapes=[pltpu.VMEM((cols, depth), jnp.bfloat16)],
        ),
        cost_estimate=pl.CostEstimate(
            flops=2 * rows * cols * depth,
            bytes_accessed=rows * cols * 8 + 2 * (rows + cols) * depth,
            transcendentals=0,
        ),
        compiler_params=pltpu.CompilerParams(vmem_limit_bytes=32 << 20),
        name="second",
    )(meta, pltpu.with_memory_space_constraint(accumulated, pltpu.HBM), gap_rows, gap_cols, *row_parts, *col_parts)


def lookup(index, table):
    hits = index[:, None] == jnp.arange(table.shape[0], dtype=jnp.int32)[None, :]
    return jnp.sum(jnp.where(hits, table[None, :], jnp.zeros((), table.dtype)), axis=1)


def narrow(value):
    return (value * SCALE).astype(jnp.float16)


def widen(value):
    return value.astype(jnp.float32) * (1.0 / SCALE)


class Shared:
    pass


class Chunk:
    def __init__(self, env, b_piece):
        self.env, self.b_piece = env, b_piece

    def S(self):
        self.skewed = send(self.b_piece, skew)

    def R(self):
        self.base = send(self.skewed, reflect)

    def Y(self):
        self.swapped = send(self.base, other_l)
        self.near = near_sends(self.base, along_z)

    def Q(self):
        self.near_swapped = near_sends(self.swapped, along_z)

    def F(self):
        across = send(self.near[1], along_z(1))
        across_swapped = send(self.near_swapped[0], along_z(-1))
        self.b_pieces = [self.base, *self.near, across, self.swapped, *self.near_swapped, across_swapped]

    def P(self):
        self.partials = first_product(self.env.meta, self.env.own, self.env.other, self.b_pieces)
        self.narrowed = [narrow(self.partials[i]) for i in range(7)]

    def M(self):
        self.arrived = [send(self.narrowed[i], along_col(*TARGETS[i])) for i in range(7)]

    def X(self):
        total = self.partials[7] + sum(widen(a) for a in self.arrived)
        self.x_piece = (self.b_piece.astype(jnp.float32) + total).astype(jnp.bfloat16)
        self.skewed = send(self.x_piece, skew)
        self.swapped = send(self.x_piece, other_h)

    def O(self):
        self.near = near_sends(self.x_piece, along_x)

    def U(self):
        self.base = send(self.skewed, reflect)

    def W(self):
        self.near_swapped = near_sends(self.swapped, along_x)

    def V(self):
        across = send(self.near[1], along_x(1))
        across_swapped = send(self.near_swapped[0], along_x(-1))
        self.row_pieces = [self.x_piece, *self.near, across, self.swapped, *self.near_swapped, across_swapped]

    def N(self):
        near = send(self.base, pass_core)
        far = send(self.base, cross_core)
        straight = self.env.l == self.env.c
        self.mine = jnp.where(straight, self.base, near)
        self.theirs = jnp.where(straight, near, far)

    def Z(self):
        self.mine_near = near_sends(self.mine, along_z)
        self.theirs_near = near_sends(self.theirs, along_z)

    def G(self):
        mine_across = send(self.mine_near[1], along_z(1))
        theirs_across = send(self.theirs_near[0], along_z(-1))
        self.env.col_mine += [self.mine, *self.mine_near, mine_across]
        self.env.col_theirs += [self.theirs, *self.theirs_near, theirs_across]

    def E(self):
        x_rows = order_rows(self.env.meta, self.row_pieces)
        self.env.row_mine.append(x_rows)
        self.env.row_theirs.append(send(x_rows, other_core))


def on_device(amplitudes, accumulated, cholesky, occ_index, vir_index, occ_energy, vir_energy):
    row_rank = lax.axis_index("row").astype(jnp.int32)
    col_rank = lax.axis_index("col").astype(jnp.int32)
    row_block, col_block = amplitudes.shape
    l, z = row_rank >> 2, row_rank & 3
    h, x, c = col_rank >> 3, (col_rank >> 1) & 3, col_rank & 1
    env = Shared()
    env.l, env.c = l, c

    swap, ring = jnp.array(SWAP_RING, jnp.int32).T
    to_h, to_x = jnp.array(TARGETS, jnp.int32).T
    destinations = (h ^ to_h) * 4 + ((x + to_x) & 3)
    sources = ((l ^ swap) * 4 + ((z + ring - x) & 3) - 4 * c) & 7
    mine = (h ^ swap) * 4 + ((x + ring) & 3)
    env.meta = jnp.concatenate([destinations, sources, mine, (z + ring - x) & 3])

    half = cholesky.shape[1] // 2
    keep = lax.dynamic_slice_in_dim(cholesky, c * half, half, 1)
    got = send(lax.dynamic_slice_in_dim(cholesky, (1 - c) * half, half, 1), other_core)
    b_piece = jnp.concatenate([jnp.where(c == 0, keep, got), jnp.where(c == 0, got, keep)], axis=0)
    env.own = amplitudes

    occ_rows = lax.dynamic_slice_in_dim(occ_index, row_rank * row_block, row_block, 0)
    vir_rows = lax.dynamic_slice_in_dim(vir_index, row_rank * row_block, row_block, 0)
    occ_cols = lax.dynamic_slice_in_dim(occ_index, col_rank * col_block, col_block, 0)
    vir_cols = lax.dynamic_slice_in_dim(vir_index, col_rank * col_block, col_block, 0)
    gap_rows = lookup(occ_rows, occ_energy) - lookup(vir_rows, vir_energy)
    gap_cols = lookup(occ_cols, occ_energy) - lookup(vir_cols, vir_energy)
    env.meta, gap_rows, gap_cols = lax.optimization_barrier(
        (env.meta, jnp.broadcast_to(gap_rows[:, None], (row_block, 128)), gap_cols[None, :])
    )

    env.row_mine, env.row_theirs, env.col_mine, env.col_theirs = [], [], [], []
    starts = [sum(WIDTHS[:j]) for j in range(len(WIDTHS))]
    chunks = [Chunk(env, b_piece[:, start : start + width]) for start, width in zip(starts, WIDTHS)]
    for stage in ORDER:
        if stage == "*":
            env.other = send(amplitudes, other_core)
        elif stage == "+":
            tied = (chunks[0].narrowed, chunks[1].near, chunks[1].near_swapped)
            chunks[0].narrowed, chunks[1].near, chunks[1].near_swapped = lax.optimization_barrier(tied)
        else:
            getattr(chunks[int(stage.islower())], stage.upper())()
    return second_product(
        env.meta, accumulated, gap_rows, gap_cols, env.row_mine + env.row_theirs, env.col_mine + env.col_theirs
    )


def solution(mesh):
    in_specs = (P("row", "col"), P("row", "col"), P(("row", "col"), None), P(), P(), P(), P())
    out_specs = P("row", "col")
    return jax.shard_map(on_device, mesh=mesh, in_specs=in_specs, out_specs=out_specs, check_vma=False)
```
